32 devices in a mesh: expert: 16 (over z, y, x), fsdp: 2 (over core).
Axes of the slice: x: 2, y: 2, z: 4, core: 2. Of those that a mesh axis runs over, the one named last changes fastest.
Arguments:
- tokens: bfloat16 [16384, 1024], P(('expert', 'fsdp')), may hold values from -6 to 6
- routes: int32 [16384, 8], P(('expert', 'fsdp')), may hold values from 0 to 15, all different within a row; in each aligned block of 512 rows (0 to 511, 512 to 1023, ...) at most 320 rows name the same one
- cotangent: bfloat16 [16384, 1024], P(('expert', 'fsdp')), may hold values from -6 to 6
- attention_gain: bfloat16 [1024], P('fsdp'), may hold values from 0.5 to 1.5
- query_weight: bfloat16 [1024, 1024], P('fsdp'), may hold values from -0.75 to 0.75
- key_weight: bfloat16 [1024, 512], P('fsdp'), may hold values from -0.75 to 0.75
- value_weight: bfloat16 [1024, 512], P('fsdp'), may hold values from -0.1875 to 0.1875
- output_weight: bfloat16 [1024, 1024], P('fsdp'), may hold values from -3 to 3
- router_weight: bfloat16 [1024, 16], P('fsdp'), may hold values from -0.09375 to 0.09375
- mixture_gain: bfloat16 [1024], P('fsdp'), may hold values from 0.5 to 1.5
- expert_gate: bfloat16 [16, 1024, 512], P('expert', 'fsdp'), may hold values from -0.1875 to 0.1875
- expert_up: bfloat16 [16, 1024, 512], P('expert', 'fsdp'), may hold values from -0.1875 to 0.1875
- expert_down: bfloat16 [16, 512, 1024], P('expert', None, 'fsdp'), may hold values from -6 to 6
Outputs:
- output: bfloat16 [16384, 1024], P(('expert', 'fsdp'))
- input_grad: float32 [16384, 1024], P(('expert', 'fsdp'))
- attention_gain_grad: float32 [1024], P('fsdp')
- query_grad: float32 [1024, 1024], P('fsdp')
- key_grad: float32 [1024, 512], P('fsdp')
- value_grad: float32 [1024, 512], P('fsdp')
- output_weight_grad: float32 [1024, 1024], P('fsdp')
- router_grad: float32 [1024, 16], P('fsdp')
- mixture_gain_grad: float32 [1024], P('fsdp')
- gate_grad: float32 [16, 1024, 512], P('expert', 'fsdp')
- up_grad: float32 [16, 1024, 512], P('expert', 'fsdp')
- down_grad: float32 [16, 512, 1024], P('expert', None, 'fsdp')
The draws below stay inside these ranges and needn't reach their ends.
Inputs may be any that keep to these rules, and one draw needn't show every extreme that they name: `routes`: each token names 8 different experts; at most 320 of the 512 tokens of one device name the same expert, a bound that some block reaches of them on some device.
All inputs are finite; a program needn't handle non-finite values.
Results may differ from the reference program's by a relative error of at most 0.023.
Values may be sent and summed in bfloat16 or wider, within the bound.
No kernel may reach another device: no remote copies, remote signals or barrier semaphores. Data moves between devices by JAX's collectives and lax.ppermute only.
A program may use at most 192 MiB of HBM per device.

```python
import math
import jax
import jax.numpy as jnp
import numpy as np
from jax import lax

D = 1024
HEADS = 16
KVH = 8
HD = 64
FFE = 512
TOP = 8
TOK_DEV = 512
EXPERTS = 16
CAP = 320
TOKENS = 16384


def level_of(rng, extent, shards, low, high):
    factor_of = 1.0
    for axis_at, parts in shards:
        heights = jax.random.uniform(jax.random.fold_in(jax.random.fold_in(rng, 6), axis_at), (parts,), jnp.float32, low / len(shards), high / len(shards))
        factor_of = factor_of * jnp.repeat(jnp.exp(heights), extent[axis_at] // parts).reshape((-1,) + (1,) * (len(extent) - 1 - axis_at))
    return factor_of


def shared_out(rng, own, number, rows, count, top, reach, lean):
    sequence = jax.random.permutation(rng, count)
    crowded, common = shares(count, rows * top, reach, lean, True), shares(count, rows * top, reach, lean, False)
    places = jnp.arange(count)

    def named(tallies, offset_by):
        used = int((tallies > 0).sum())
        fixed = max(1, used // 4)
        moved = fixed + (places - fixed + offset_by * (used - fixed)) % max(1, count - fixed)
        return jnp.zeros((count,), jnp.int32).at[sequence[jnp.where(places < fixed, places, moved)]].set(jnp.asarray(tallies, jnp.int32))

    tallies = jnp.where(number % 4 == 0, named(crowded, number // 4), named(common, number - number // 4 - 1))
    mixed = jax.random.permutation(jax.random.fold_in(own, 3), count)
    source_of, sink = mixed[0:count // 2 * 2:2], mixed[1:count // 2 * 2:2]
    slack = jnp.minimum(tallies[source_of] - 1, reach - tallies[sink]) // 2
    slack = jnp.where((source_of == sequence[0]) | (sink == sequence[0]) | (tallies[sink] == 0), 0, jnp.maximum(slack, 0))
    moved = jax.random.randint(jax.random.fold_in(own, 4), (count // 2,), 0, 1 << 20) % (slack + 1)
    tallies = tallies.at[source_of].add(-moved).at[sink].add(moved)
    members = jnp.searchsorted(jnp.cumsum(tallies), jnp.arange(rows * top), side="right").astype(jnp.int32)
    grid = members.reshape(top, rows).T
    grid = grid[jax.random.permutation(jax.random.fold_in(own, 1), rows)]
    offset_by = jax.random.randint(jax.random.fold_in(own, 2), (rows, 1), 0, top)
    return jnp.take_along_axis(grid, (jnp.arange(top)[None, :] + offset_by) % top, axis=1)


def shares(count, total, bound, lean, full):
    weights = [(1 << 20) // math.isqrt(grade ** lean) + 1 for grade in range(1, count + 1)]
    largest = bound if full else min(bound, max(-(-total // count), total * weights[0] // sum(weights)))
    least = 1 if total - largest >= count - 1 else 0
    holding, surplus = [largest] + [least] * (count - 1), total - largest - least * (count - 1)
    while surplus > 0:
        candidates = [i for i in range(1, count) if holding[i] < largest] or [i for i in range(1, count) if holding[i] < bound]
        pool, remaining = sum([weights[i] for i in candidates]), surplus
        for i in candidates:
            more = min(bound - holding[i], max(1, remaining * weights[i] // pool), surplus)
            holding[i] = holding[i] + more
            surplus = surplus - more
    return np.array(holding)


def centred(key, shape, deviation, most, split=(), kind=jnp.bfloat16):
    drawn = deviation * jax.random.normal(key, shape, jnp.float32)
    if split:
        drawn = drawn * level_of(key, shape, split, -0.22, 0.18)
    return jnp.clip(drawn, -most, most).astype(kind)


def setup_inputs(seed: int = 0) -> dict:
    keys = jax.random.split(jax.random.key(seed), 14)
    tokens = centred(keys[0], (TOKENS, D), 1.0, 6.0, ((0, 32),))
    routes_keys = jax.random.split(jax.random.fold_in(keys[1], 1), TOKENS // TOK_DEV)
    routes_turns = jax.random.permutation(jax.random.fold_in(keys[1], 3), TOKENS // TOK_DEV)
    routes = jax.vmap(lambda own, number: shared_out(jax.random.fold_in(keys[1], 2), own, number, TOK_DEV, EXPERTS, TOP, CAP, 1))(routes_keys, routes_turns).reshape((TOKENS, TOP))
    cotangent = centred(keys[2], (TOKENS, D), 1.0, 6.0, ((0, 32),))
    attention_gain = jnp.clip(1.0 + 0.1 * jax.random.normal(keys[3], (D,), jnp.float32), 0.5, 1.5).astype(jnp.bfloat16)
    query_weight = centred(keys[4], (D, HEADS * HD), HD ** -0.5, 0.75, ((0, 2),))
    key_weight = centred(keys[5], (D, KVH * HD), HD ** -0.5, 0.75, ((0, 2),))
    value_weight = centred(keys[6], (D, KVH * HD), D ** -0.5, 0.1875, ((0, 2),))
    output_weight = centred(keys[7], (HEADS * HD, D), 4 ** -0.5, 3.0, ((0, 2),))
    router_weight = centred(keys[8], (D, EXPERTS), (4 * D) ** -0.5, 0.09375, ((0, 2),))
    mixture_gain = jnp.clip(1.0 + 0.1 * jax.random.normal(keys[9], (D,), jnp.float32), 0.5, 1.5).astype(jnp.bfloat16)
    expert_gate = centred(keys[10], (EXPERTS, D, FFE), D ** -0.5, 0.1875, ((0, 16), (1, 2)))
    expert_up = centred(keys[11], (EXPERTS, D, FFE), D ** -0.5, 0.1875, ((0, 16), (1, 2)))
    expert_down = centred(keys[12], (EXPERTS, FFE, D), 1 ** -0.5, 6.0, ((0, 16), (2, 2)))
    return dict(tokens=tokens, routes=routes, cotangent=cotangent, attention_gain=attention_gain, query_weight=query_weight, key_weight=key_weight, value_weight=value_weight, output_weight=output_weight, router_weight=router_weight, mixture_gain=mixture_gain, expert_gate=expert_gate, expert_up=expert_up, expert_down=expert_down)


RESIDUAL_SCALE = 0.22
ATTENTION_SCALE = 0.015625
NORM_EPS = 1e-06
ROPE_BASE = 10000.0
HIGHEST = lax.Precision.HIGHEST

@jax.custom_vjp
def low(v):
    return lax.optimization_barrier(v.astype(jnp.bfloat16)).astype(jnp.float32)

@jax.custom_vjp
def low_back(v):
    return v

def low_keep(v):
    return (low(v), None)

def low_pass(kept, grad):
    return (grad,)

def back_keep(v):
    return (v, None)

def back_low(kept, grad):
    return (low(grad),)
low.defvjp(low_keep, low_pass)
low_back.defvjp(back_keep, back_low)

def rotary_tables(seq_len):
    half_size = HD // 2
    frequency = ROPE_BASE ** (-(jnp.arange(half_size).astype(jnp.float32) * 2.0 / HD))
    angles = jnp.arange(seq_len).astype(jnp.float32)[:, None] * frequency[None, :]
    angles = jnp.concatenate([angles, angles], axis=1)
    return (jnp.cos(angles), jnp.sin(angles))

def rotate(values, cosine, sine_table):
    half_size = values.shape[-1] // 2
    turned = jnp.concatenate([-values[..., half_size:], values[..., :half_size]], axis=-1)
    return values * cosine[:, None, :] + turned * sine_table[:, None, :]

def slot_tables(routes, expert_total, capacity):
    seq_len, pick_count = routes.shape
    flat_routes = routes.reshape(-1)
    one_hot = (flat_routes[:, None] == jnp.arange(expert_total).astype(jnp.int32)[None, :]).astype(jnp.int32)
    before = (jnp.cumsum(one_hot, axis=0) - one_hot).astype(jnp.int32)
    pair_rank = lax.optimization_barrier(jnp.sum(before * one_hot, axis=1)).astype(jnp.int32)
    slot_index = (flat_routes * capacity + pair_rank).astype(jnp.int32)
    pair_total = seq_len * pick_count
    slot_source = jnp.full((expert_total * capacity,), pair_total, jnp.int32)
    slot_source = slot_source.at[slot_index].set(jnp.arange(pair_total).astype(jnp.int32))
    return (slot_index, slot_source)

def block_forward(params, inputs, routes):
    attention_gain, query_weight, key_weight, value_weight, output_weight, router_weight, mixture_gain, expert_gate, expert_up, expert_down = params
    seq_len = inputs.shape[0]
    scale_one = lax.rsqrt(lax.optimization_barrier(jnp.mean(inputs * inputs, axis=1, keepdims=True)) + NORM_EPS)
    normed_one = low(inputs * scale_one * attention_gain)
    cosine, sine_table = rotary_tables(seq_len)
    query_lin = low_back(jnp.dot(normed_one, query_weight, precision=HIGHEST)).reshape(seq_len, HEADS, HD)
    key_lin = low_back(jnp.dot(normed_one, key_weight, precision=HIGHEST)).reshape(seq_len, KVH, HD)
    value_rows = low(low_back(jnp.dot(normed_one, value_weight, precision=HIGHEST))).reshape(seq_len, KVH, HD)
    query_rot = low(rotate(query_lin, cosine, sine_table)).reshape(seq_len, KVH, HEADS // KVH, HD)
    key_rot = low(rotate(key_lin, cosine, sine_table))
    raw_scores = low_back(jnp.einsum('qgrd,kgd->grqk', query_rot, key_rot, precision=HIGHEST))
    causal = jnp.arange(seq_len)[:, None] >= jnp.arange(seq_len)[None, :]
    scores = jnp.where(causal, raw_scores * ATTENTION_SCALE, -1e+30)
    weights = low(jax.nn.softmax(scores, axis=-1))
    mixed = low(low_back(jnp.einsum('grqk,kgd->qgrd', weights, value_rows, precision=HIGHEST)))
    attention_out = low_back(jnp.dot(mixed.reshape(seq_len, HEADS * HD), output_weight, precision=HIGHEST))
    middle = inputs + RESIDUAL_SCALE * attention_out
    scale_two = lax.rsqrt(lax.optimization_barrier(jnp.mean(middle * middle, axis=1, keepdims=True)) + NORM_EPS)
    normed_two = low(middle * scale_two * mixture_gain)
    logits = jnp.dot(normed_two, router_weight, precision=HIGHEST)
    chosen = (routes[:, :, None] == jnp.arange(EXPERTS).astype(jnp.int32)[None, None, :]).astype(jnp.float32)
    picked = jnp.einsum('tke,te->tk', chosen, logits, precision=HIGHEST)
    gate_weights = jax.nn.softmax(picked, axis=-1)
    slot_index, slot_source = slot_tables(routes, EXPERTS, CAP)
    pair_rows = low_back(jnp.repeat(normed_two, TOP, axis=0))
    padded = jnp.concatenate([pair_rows, jnp.zeros((1, D), jnp.float32)], axis=0)
    expert_in = padded[slot_source].reshape(EXPERTS, CAP, D)
    gate_pre = low_back(jnp.einsum('ecd,edf->ecf', expert_in, expert_gate, precision=HIGHEST))
    up_pre = low_back(jnp.einsum('ecd,edf->ecf', expert_in, expert_up, precision=HIGHEST))
    hidden_act = low(jax.nn.silu(gate_pre) * up_pre)
    produced = low(low_back(jnp.einsum('ecf,efd->ecd', hidden_act, expert_down, precision=HIGHEST)))
    pair_out = produced.reshape(EXPERTS * CAP, D)[slot_index].reshape(seq_len, TOP, D)
    mixture = lax.optimization_barrier(jnp.sum(gate_weights[:, :, None] * pair_out, axis=1))
    return middle + RESIDUAL_SCALE * mixture

def reference(tokens, routes, cotangent, attention_gain, query_weight, key_weight, value_weight, output_weight, router_weight, mixture_gain, expert_gate, expert_up, expert_down):
    params = tuple((weight_array.astype(jnp.float32) for weight_array in (attention_gain, query_weight, key_weight, value_weight, output_weight, router_weight, mixture_gain, expert_gate, expert_up, expert_down)))
    blocks = tokens.astype(jnp.float32).reshape(-1, TOK_DEV, D)
    route_blocks = routes.reshape(-1, TOK_DEV, TOP)

    def whole_pass(params, blocks):

        def scan_step(running, pieces):
            return (running, block_forward(params, pieces[0], pieces[1]))
        return lax.scan(jax.checkpoint(scan_step), jnp.zeros((), jnp.float32), (blocks, route_blocks))[1]
    result, pullback = jax.vjp(whole_pass, params, blocks)
    gradients, grad_blocks = pullback(cotangent.astype(jnp.float32).reshape(result.shape))
    return (result.reshape(TOKENS, D).astype(jnp.bfloat16), grad_blocks.reshape(TOKENS, D), gradients[0], gradients[1], gradients[2], gradients[3], gradients[4], gradients[5], gradients[6], gradients[7], gradients[8], gradients[9])
```

```python
from functools import partial

import jax
import jax.numpy as jnp
from jax import lax
from jax.sharding import PartitionSpec as P

HD = 64
OUTER = 4

RESIDUAL_SCALE = 0.22
ATTENTION_SCALE = 0.015625
NORM_EPS = 1e-06
ROPE_BASE = 10000.0
HIGHEST = lax.Precision.HIGHEST
BF = jnp.bfloat16
F32 = jnp.float32


def dot(a, b, lhs=1, rhs=0):
    return lax.dot_general(a, b, (((lhs,), (rhs,)), ((), ())), preferred_element_type=F32)


class Net:
    def __init__(self):
        self.experts = lax.axis_size("expert")
        self.parts = lax.axis_size("fsdp")
        self.inner = self.experts // OUTER
        index = lax.axis_index("expert")
        self.outer_at = index // self.inner
        self.inner_at = index % self.inner
        self.part_at = lax.axis_index("fsdp")

    def plane_move(self, value, flip):
        pairs = [
            (o * self.inner + i, o * self.inner + (i ^ flip))
            for o in range(OUTER)
            for i in range(self.inner)
        ]
        return lax.ppermute(value, "expert", pairs)

    def line_move(self, value, hops):
        pairs = [
            (a * self.inner + i, b * self.inner + i) for a, b in hops for i in range(self.inner)
        ]
        return lax.ppermute(value, "expert", pairs)

    def swap(self, value):
        return lax.ppermute(value, "fsdp", [(0, 1), (1, 0)])

    def gather_plane(self, value):
        if self.inner != 4:
            return [value] + [self.plane_move(value, flip) for flip in range(1, self.inner)]
        half = value.shape[0] // 2
        across = self.plane_move(value, 1)
        along = self.plane_move(value, 2)
        top = self.plane_move(along[:half], 1)
        bottom = self.plane_move(across[half:], 2)
        return [value, across, along, jnp.concatenate([top, bottom], axis=0)]

    def scatter_plane(self, blocks):
        if self.inner != 4:
            total = blocks[0].astype(F32)
            for flip in range(1, self.inner):
                total = total + self.plane_move(blocks[flip], flip).astype(F32)
            return total
        own, across, along, far = blocks
        half = own.shape[0] // 2
        for_along = self.plane_move(far[:half], 1)
        for_across = self.plane_move(far[half:], 2)
        across = jnp.concatenate([across[:half], across[half:] + for_across], axis=0)
        along = jnp.concatenate([along[:half] + for_along, along[half:]], axis=0)
        first = self.plane_move(across, 1)
        second = self.plane_move(along, 2)
        return own.astype(F32) + first.astype(F32) + second.astype(F32)

    def middle_at(self):
        return (self.outer_at == 1) | (self.outer_at == 2)

    def gather_line(self, value):
        near = self.line_move(value, [(0, 1), (1, 0), (2, 3), (3, 2)])
        inside = self.line_move(value, [(1, 2), (2, 1)])
        far_inside = self.line_move(near, [(1, 2), (2, 1)])
        edge = self.line_move(inside, [(1, 0), (2, 3)])
        far_edge = self.line_move(far_inside, [(1, 0), (2, 3)])
        middle = self.middle_at()
        following = jnp.where(middle, inside, edge)
        far = jnp.where(middle, far_inside, far_edge)
        return [value, near, following, far]

    def line_order(self):
        following = jnp.where(self.outer_at < 2, 2, 1)
        far = jnp.where(self.outer_at < 2, 3, 0)
        return [self.outer_at, self.outer_at ^ 1, following, far]

    def scatter_line(self, own, near, following, far):
        from_edge = self.line_move(far, [(0, 1), (3, 2)])
        far = far + from_edge
        crossing = self.line_move(far, [(1, 2), (2, 1)])
        outside = self.line_move(following, [(0, 1), (3, 2)])
        inside = self.line_move(following + outside, [(1, 2), (2, 1)])
        beside = self.line_move(near + crossing, [(0, 1), (1, 0), (2, 3), (3, 2)])
        return own.astype(F32) + inside.astype(F32) + beside.astype(F32)

    def gather_parts(self, value, axis):
        if self.parts != 2:
            return lax.all_gather(value, "fsdp", axis=axis, tiled=True)
        other = self.swap(value)
        first = self.part_at == 0
        return jnp.concatenate(
            [jnp.where(first, value, other), jnp.where(first, other, value)], axis=axis
        )

    def scatter_parts(self, value, axis):
        if self.parts != 2:
            return lax.psum_scatter(value, "fsdp", scatter_dimension=axis, tiled=True)
        half = value.shape[axis] // 2
        kept = lax.dynamic_slice_in_dim(value, self.part_at * half, half, axis)
        sent = lax.dynamic_slice_in_dim(value, (1 - self.part_at) * half, half, axis)
        return kept + self.swap(sent.astype(BF)).astype(value.dtype)

    def halve(self, value, flip, bit):
        half = value.shape[0] // 2
        kept = lax.dynamic_slice_in_dim(value, bit * half, half, 0)
        sent = lax.dynamic_slice_in_dim(value, (1 - bit) * half, half, 0)
        return kept + self.plane_move(sent, flip)

    def unhalve(self, value, flip, bit):
        other = self.plane_move(value, flip)
        first = bit == 0
        return jnp.concatenate(
            [jnp.where(first, value, other), jnp.where(first, other, value)], axis=0
        )

    def line_sum(self, value):
        rows = value.shape[0] // 4

        def hops(flip):
            return [(a, a ^ flip) for a in range(4)]

        total = lax.dynamic_slice_in_dim(value, self.outer_at * rows, rows, 0)
        for flip in (1, 2, 3):
            piece = lax.dynamic_slice_in_dim(value, (self.outer_at ^ flip) * rows, rows, 0)
            total = total + self.line_move(piece, hops(flip))
        pieces = [total] + [self.line_move(total, hops(flip)) for flip in (1, 2, 3)]
        low, high = self.outer_at % 2 == 0, self.outer_at < 2
        first = [jnp.where(low, pieces[0], pieces[1]), jnp.where(low, pieces[1], pieces[0])]
        second = [jnp.where(low, pieces[2], pieces[3]), jnp.where(low, pieces[3], pieces[2])]
        first, second = jnp.concatenate(first, axis=0), jnp.concatenate(second, axis=0)
        return jnp.concatenate(
            [jnp.where(high, first, second), jnp.where(high, second, first)], axis=0
        )

    def sum_experts(self, value):
        if self.experts != 16:
            return lax.psum(value, "expert")
        columns = value.shape[1] // 2
        x_bit, y_bit = self.inner_at % 2, self.inner_at // 2
        first = self.halve(value[:, :columns], 1, x_bit)
        second = self.halve(value[:, columns:], 2, y_bit)
        first = self.halve(first, 2, y_bit)
        second = self.halve(second, 1, x_bit)
        both = self.line_sum(jnp.concatenate([first, second], axis=1))
        first, second = both[:, :columns], both[:, columns:]
        first = self.unhalve(self.unhalve(first, 2, y_bit), 1, x_bit)
        second = self.unhalve(self.unhalve(second, 1, x_bit), 2, y_bit)
        return jnp.concatenate([first, second], axis=1)

    def sum_small(self, value):
        if self.experts != 16:
            return lax.psum(value, "expert")
        value = value + self.plane_move(value, 1)
        value = value + self.plane_move(value, 2)
        value = value + self.line_move(value, [(a, a ^ 1) for a in range(4)])
        return value + self.line_move(value, [(a, a ^ 2) for a in range(4)])


def rotary_tables(seq_len):
    half_size = HD // 2
    frequency = ROPE_BASE ** (-(jnp.arange(half_size).astype(F32) * 2.0 / HD))
    angles = jnp.arange(seq_len).astype(F32)[:, None] * frequency[None, :]
    angles = jnp.concatenate([angles, angles], axis=1)
    return (jnp.cos(angles), jnp.sin(angles))


def rotate(values, cosine, sine_table):
    half_size = values.shape[-1] // 2
    turned = jnp.concatenate([-values[..., half_size:], values[..., :half_size]], axis=-1)
    return values * cosine[:, None, :] + turned * sine_table[:, None, :]


def rotate_back(values, cosine, sine_table):
    half_size = values.shape[-1] // 2
    scaled = values * sine_table[:, None, :]
    turned = jnp.concatenate([scaled[..., half_size:], -scaled[..., :half_size]], axis=-1)
    return values * cosine[:, None, :] + turned


def group_forward(causal, operands):
    query_block, key_block, value_block = operands
    raw_scores = jnp.einsum(
        "qrd,kd->rqk", query_block, key_block, preferred_element_type=jnp.float32
    )
    scores = jnp.where(causal, raw_scores * ATTENTION_SCALE, -1e30)
    row_max = jnp.max(scores, axis=-1, keepdims=True)
    shifted = jnp.exp(scores - row_max)
    row_total = jnp.sum(shifted, axis=-1, keepdims=True)
    weights = (shifted / row_total).astype(jnp.bfloat16)
    mixed = jnp.einsum("rqk,kd->qrd", weights, value_block, preferred_element_type=jnp.float32)
    return (mixed.astype(jnp.bfloat16), row_max + jnp.log(row_total))


def group_backward(causal, operands):
    query_block, key_block, value_block, log_total, grad_block = operands
    raw_scores = jnp.einsum(
        "qrd,kd->rqk", query_block, key_block, preferred_element_type=jnp.float32
    )
    scores = jnp.where(causal, raw_scores * ATTENTION_SCALE, -1e30)
    weights = jnp.exp(scores - log_total)
    grad_weights = jnp.einsum(
        "qrd,kd->rqk", grad_block, value_block, preferred_element_type=jnp.float32
    )
    row_inner = jnp.sum(weights * grad_weights, axis=-1, keepdims=True)
    grad_raw = (weights * (grad_weights - row_inner) * ATTENTION_SCALE).astype(jnp.bfloat16)
    grad_query = jnp.einsum("rqk,kd->qrd", grad_raw, key_block, preferred_element_type=jnp.float32)
    grad_key = jnp.einsum("rqk,qrd->kd", grad_raw, query_block, preferred_element_type=jnp.float32)
    grad_value = jnp.einsum(
        "rqk,qrd->kd", weights.astype(jnp.bfloat16), grad_block, preferred_element_type=jnp.float32
    )
    return (grad_query, grad_key, grad_value)


def body(
    tokens,
    routes,
    cotangent,
    attention_gain,
    query_weight,
    key_weight,
    value_weight,
    output_weight,
    router_weight,
    mixture_gain,
    expert_gate,
    expert_up,
    expert_down,
):
    net = Net()
    seq_len, model_width = tokens.shape
    expert_total = router_weight.shape[1]
    hidden_width = expert_gate.shape[2]
    inner_total = query_weight.shape[1]
    key_total = key_weight.shape[1]

    projections = jnp.concatenate([query_weight, key_weight, value_weight], axis=1)
    weight_qkv = net.gather_parts(projections, 0)
    weight_output = net.gather_parts(output_weight, 0)
    small = jnp.concatenate(
        [
            router_weight.astype(F32).T,
            attention_gain.astype(F32)[None],
            mixture_gain.astype(F32)[None],
        ],
        axis=0,
    )
    small = net.gather_parts(small, 1)
    router_wide = small[:expert_total].T
    weight_router = router_wide.astype(BF)
    gain_one, gain_two = small[expert_total], small[expert_total + 1]

    gate_up = jnp.concatenate([expert_gate[0], expert_up[0]], axis=1)
    line_gate_up = net.gather_line(gate_up)
    line_down = net.gather_line(expert_down[0])
    grad_blocks = net.gather_plane(cotangent)

    inputs = tokens.astype(F32)
    scale_one = lax.rsqrt(jnp.mean(inputs * inputs, axis=1, keepdims=True) + NORM_EPS)
    unit_one = inputs * scale_one
    normed_one = (unit_one * gain_one).astype(BF)
    cosine, sine_table = rotary_tables(seq_len)
    kv_heads = key_total // HD
    group_size = inner_total // key_total
    qkv = dot(normed_one, weight_qkv)
    query_lin = qkv[:, :inner_total].reshape(seq_len, -1, HD)
    key_lin = qkv[:, inner_total : inner_total + key_total].reshape(seq_len, -1, HD)
    value_rows = qkv[:, inner_total + key_total :].astype(BF)
    query_rot = rotate(query_lin, cosine, sine_table).astype(BF)
    key_rot = rotate(key_lin, cosine, sine_table).astype(BF)
    query_groups = query_rot.reshape(seq_len, kv_heads, group_size, HD).transpose(1, 0, 2, 3)
    key_groups = key_rot.transpose(1, 0, 2)
    value_groups = value_rows.reshape(seq_len, kv_heads, HD).transpose(1, 0, 2)
    causal = jnp.arange(seq_len)[:, None] >= jnp.arange(seq_len)[None, :]
    mixed_groups, log_totals = lax.map(
        partial(group_forward, causal), (query_groups, key_groups, value_groups)
    )
    mixed = mixed_groups.transpose(1, 0, 2, 3).reshape(seq_len, -1)
    middle = inputs + RESIDUAL_SCALE * dot(mixed, weight_output)
    scale_two = lax.rsqrt(jnp.mean(middle * middle, axis=1, keepdims=True) + NORM_EPS)
    unit_two = middle * scale_two
    normed_two = (unit_two * gain_two).astype(BF)
    row_blocks = net.gather_plane(normed_two)

    logits = dot(weight_router, normed_two, 0, 1)
    chosen = jnp.any(
        routes.T[None] == jnp.arange(expert_total)[:, None, None], axis=1
    )
    shifted = jnp.where(chosen, logits, -1e30)
    shifted = jnp.where(chosen, jnp.exp(shifted - jnp.max(shifted, axis=0, keepdims=True)), 0.0)
    gates = shifted / jnp.sum(shifted, axis=0, keepdims=True)
    gate_blocks = [gates] + [net.plane_move(gates, flip) for flip in range(1, net.inner)]

    order = net.line_order()
    rows = jnp.concatenate(row_blocks, axis=0)
    grads = jnp.concatenate(grad_blocks, axis=0)
    gate_columns = jnp.stack(
        [
            jnp.concatenate(
                [
                    lax.dynamic_index_in_dim(
                        block, at * net.inner + net.inner_at, 0, keepdims=False
                    )
                    for block in gate_blocks
                ]
            )
            for at in order
        ]
    )
    mixture, grad_rows, grad_gates, grad_weights = 0.0, 0.0, [], []
    for at in range(OUTER):
        weight_gate_up = net.gather_parts(line_gate_up[at], 0)
        weight_down = net.gather_parts(line_down[at], 1)
        pre = dot(rows, weight_gate_up)
        gate_pre, up_pre = pre[:, :hidden_width], pre[:, hidden_width:]
        back = dot(grads, weight_down, 1, 1)
        sigmoid = jax.nn.sigmoid(gate_pre)
        active = gate_pre * sigmoid
        hidden = active * up_pre
        factor = RESIDUAL_SCALE * gate_columns[at][:, None]
        grad_gates.append(RESIDUAL_SCALE * jnp.sum(hidden * back, axis=1))
        scaled = (hidden * factor).astype(BF)
        mixture = mixture + dot(scaled, weight_down)
        back = back * factor
        grad_pre = jnp.concatenate(
            [
                (back * up_pre * sigmoid * (1.0 + gate_pre * (1.0 - sigmoid))).astype(BF),
                (back * active).astype(BF),
            ],
            axis=1,
        )
        grad_rows = grad_rows + dot(grad_pre, weight_gate_up, 1, 1)
        grad_weights.append(
            (
                net.scatter_parts(dot(rows, grad_pre, 0, 0).astype(BF), 0),
                net.scatter_parts(dot(scaled, grads, 0, 0).astype(BF), 1),
            )
        )
        if net.inner != 4:
            rows, grads, mixture, grad_rows, grad_weights = lax.optimization_barrier(
                (rows, grads, mixture, grad_rows, grad_weights)
            )
    mixture = mixture.astype(BF)
    grad_rows = grad_rows.astype(BF)

    def split(value):
        return [value[at * seq_len : (at + 1) * seq_len] for at in range(net.inner)]

    grad_normed_two = net.scatter_plane(split(grad_rows))
    added = net.scatter_plane(split(mixture))
    grad_gate_up = net.scatter_line(*[pair[0] for pair in grad_weights])
    grad_down = net.scatter_line(*[pair[1] for pair in grad_weights])

    gate_terms = jnp.stack(grad_gates).reshape(OUTER, net.inner, seq_len)
    places = jnp.stack(order)
    by_outer = jnp.zeros_like(gate_terms).at[places].set(gate_terms)
    received = [by_outer[:, 0]] + [
        net.plane_move(by_outer[:, flip], flip) for flip in range(1, net.inner)
    ]
    received = jnp.stack(received, axis=1)
    flips = jnp.arange(net.inner) ^ net.inner_at
    gate_grads = received[:, flips].reshape(expert_total, seq_len)
    grad_logits = gates * (gate_grads - jnp.sum(gates * gate_grads, axis=0, keepdims=True))
    output = (middle + added).astype(BF)

    grad_out = cotangent.astype(F32)
    grad_normed_two = grad_normed_two + lax.dot_general(
        grad_logits, router_wide, (((0,), (1,)), ((), ())), precision=HIGHEST
    )
    grad_router = lax.dot_general(
        grad_logits, normed_two.astype(F32), (((1,), (0,)), ((), ())), precision=HIGHEST
    )
    grad_unit_two = grad_normed_two * gain_two
    grad_gain_two = jnp.sum(grad_normed_two * unit_two, axis=0)
    grad_middle = grad_out + scale_two * (
        grad_unit_two - unit_two * jnp.mean(grad_unit_two * unit_two, axis=1, keepdims=True)
    )
    grad_attention = (RESIDUAL_SCALE * grad_middle).astype(BF)
    grad_output_weight = dot(mixed, grad_attention, 0, 0).astype(BF)
    total_output = net.sum_experts(net.scatter_parts(grad_output_weight, 0))
    grad_mixed = dot(grad_attention, weight_output, 1, 1).astype(BF)
    grad_mixed_groups = grad_mixed.reshape(seq_len, kv_heads, group_size, HD).transpose(1, 0, 2, 3)
    grad_query_groups, grad_key_groups, grad_value_groups = lax.map(
        partial(group_backward, causal),
        (query_groups, key_groups, value_groups, log_totals, grad_mixed_groups),
    )
    grad_query_rot = grad_query_groups.transpose(1, 0, 2, 3).reshape(seq_len, -1, HD)
    grad_query = rotate_back(grad_query_rot, cosine, sine_table).reshape(seq_len, -1).astype(BF)
    grad_key = (
        rotate_back(grad_key_groups.transpose(1, 0, 2), cosine, sine_table)
        .reshape(seq_len, -1)
        .astype(BF)
    )
    grad_value = grad_value_groups.transpose(1, 0, 2).reshape(seq_len, -1).astype(BF)
    grad_qkv = jnp.concatenate([grad_query, grad_key, grad_value], axis=1)
    grad_qkv_weight = dot(normed_one, grad_qkv, 0, 0).astype(BF)
    total_qkv = net.sum_experts(net.scatter_parts(grad_qkv_weight, 0))
    grad_normed_one = dot(grad_qkv, weight_qkv, 1, 1)
    grad_unit_one = grad_normed_one * gain_one
    grad_gain_one = jnp.sum(grad_normed_one * unit_one, axis=0)
    grad_inputs = grad_middle + scale_one * (
        grad_unit_one - unit_one * jnp.mean(grad_unit_one * unit_one, axis=1, keepdims=True)
    )
    small_grads = jnp.concatenate([grad_router, grad_gain_one[None], grad_gain_two[None]], axis=0)
    small_grads = net.sum_small(net.scatter_parts(small_grads, 1))
    return (
        output,
        grad_inputs,
        small_grads[expert_total],
        total_qkv[:, :inner_total].astype(F32),
        total_qkv[:, inner_total : inner_total + key_total].astype(F32),
        total_qkv[:, inner_total + key_total :].astype(F32),
        total_output.astype(F32),
        small_grads[:expert_total].T,
        small_grads[expert_total + 1],
        grad_gate_up[None, :, :hidden_width],
        grad_gate_up[None, :, hidden_width:],
        grad_down[None],
    )


def solution(mesh):
    both, one = P(("expert", "fsdp"), None), P("fsdp", None)
    rows, columns = P("expert", "fsdp", None), P("expert", None, "fsdp")
    return jax.shard_map(
        body,
        mesh=mesh,
        in_specs=(both, both, both, P("fsdp"), one, one, one, one, one, P("fsdp"), rows, rows, columns),
        out_specs=(both, both, P("fsdp"), one, one, one, one, one, P("fsdp"), rows, rows, columns),
        check_vma=False,
    )
```

```python
from functools import partial

import jax
import jax.numpy as jnp
from jax import lax
from jax.experimental import pallas as pl
from jax.experimental.pallas import tpu as pltpu
from jax.sharding import PartitionSpec as P

HD = 64
OUTER = 4

RESIDUAL_SCALE = 0.22
ATTENTION_SCALE = 0.015625
NORM_EPS = 1e-06
ROPE_BASE = 10000.0
HIGHEST = lax.Precision.HIGHEST
BF = jnp.bfloat16
F32 = jnp.float32


def dot(a, b, lhs=1, rhs=0):
    return lax.dot_general(a, b, (((lhs,), (rhs,)), ((), ())), preferred_element_type=F32)


class Net:
    def __init__(self):
        self.experts = lax.axis_size("expert")
        self.parts = lax.axis_size("fsdp")
        self.inner = self.experts // OUTER
        index = lax.axis_index("expert")
        self.outer_at = index // self.inner
        self.inner_at = index % self.inner
        self.part_at = lax.axis_index("fsdp")

    def plane_move(self, value, flip):
        pairs = [
            (o * self.inner + i, o * self.inner + (i ^ flip))
            for o in range(OUTER)
            for i in range(self.inner)
        ]
        return lax.ppermute(value, "expert", pairs)

    def line_move(self, value, hops):
        pairs = [
            (a * self.inner + i, b * self.inner + i) for a, b in hops for i in range(self.inner)
        ]
        return lax.ppermute(value, "expert", pairs)

    def swap(self, value):
        return lax.ppermute(value, "fsdp", [(0, 1), (1, 0)])

    def gather_plane(self, value):
        if self.inner != 4:
            return [value] + [self.plane_move(value, flip) for flip in range(1, self.inner)]
        half = value.shape[0] // 2
        across = self.plane_move(value, 1)
        along = self.plane_move(value, 2)
        top = self.plane_move(along[:half], 1)
        bottom = self.plane_move(across[half:], 2)
        return [value, across, along, jnp.concatenate([top, bottom], axis=0)]

    def scatter_plane(self, blocks):
        if self.inner != 4:
            total = blocks[0].astype(F32)
            for flip in range(1, self.inner):
                total = total + self.plane_move(blocks[flip], flip).astype(F32)
            return total
        own, across, along, far = blocks
        half = own.shape[0] // 2
        for_along = self.plane_move(far[:half], 1)
        for_across = self.plane_move(far[half:], 2)
        across = jnp.concatenate([across[:half], across[half:] + for_across], axis=0)
        along = jnp.concatenate([along[:half] + for_along, along[half:]], axis=0)
        first = self.plane_move(across, 1)
        second = self.plane_move(along, 2)
        return own.astype(F32) + first.astype(F32) + second.astype(F32)

    def middle_at(self):
        return (self.outer_at == 1) | (self.outer_at == 2)

    def gather_line(self, value):
        near = self.line_move(value, [(0, 1), (1, 0), (2, 3), (3, 2)])
        inside = self.line_move(value, [(1, 2), (2, 1)])
        far_inside = self.line_move(near, [(1, 2), (2, 1)])
        edge = self.line_move(inside, [(1, 0), (2, 3)])
        far_edge = self.line_move(far_inside, [(1, 0), (2, 3)])
        middle = self.middle_at()
        following = jnp.where(middle, inside, edge)
        far = jnp.where(middle, far_inside, far_edge)
        return [value, near, following, far]

    def line_order(self):
        following = jnp.where(self.outer_at < 2, 2, 1)
        far = jnp.where(self.outer_at < 2, 3, 0)
        return [self.outer_at, self.outer_at ^ 1, following, far]

    def scatter_line(self, own, near, following, far):
        from_edge = self.line_move(far, [(0, 1), (3, 2)])
        far = far + from_edge
        crossing = self.line_move(far, [(1, 2), (2, 1)])
        outside = self.line_move(following, [(0, 1), (3, 2)])
        inside = self.line_move(following + outside, [(1, 2), (2, 1)])
        beside = self.line_move(near + crossing, [(0, 1), (1, 0), (2, 3), (3, 2)])
        return own.astype(F32) + inside.astype(F32) + beside.astype(F32)

    def gather_parts(self, value, axis):
        if self.parts != 2:
            return lax.all_gather(value, "fsdp", axis=axis, tiled=True)
        other = self.swap(value)
        first = self.part_at == 0
        return jnp.concatenate(
            [jnp.where(first, value, other), jnp.where(first, other, value)], axis=axis
        )

    def halves(self, value, axis):
        if self.parts == 2:
            return value, self.swap(value)
        whole = lax.all_gather(value, "fsdp", axis=axis, tiled=True)
        return jnp.split(whole, 2, axis=axis)

    def scatter_parts(self, value, axis):
        if self.parts != 2:
            return lax.psum_scatter(value, "fsdp", scatter_dimension=axis, tiled=True)
        half = value.shape[axis] // 2
        kept = lax.dynamic_slice_in_dim(value, self.part_at * half, half, axis)
        sent = lax.dynamic_slice_in_dim(value, (1 - self.part_at) * half, half, axis)
        return kept + self.swap(sent.astype(BF)).astype(value.dtype)

    def halve(self, value, flip, bit):
        half = value.shape[0] // 2
        kept = lax.dynamic_slice_in_dim(value, bit * half, half, 0)
        sent = lax.dynamic_slice_in_dim(value, (1 - bit) * half, half, 0)
        return kept + self.plane_move(sent, flip)

    def unhalve(self, value, flip, bit):
        other = self.plane_move(value, flip)
        first = bit == 0
        return jnp.concatenate(
            [jnp.where(first, value, other), jnp.where(first, other, value)], axis=0
        )

    def line_sum(self, value):
        rows = value.shape[0] // 4

        def hops(flip):
            return [(a, a ^ flip) for a in range(4)]

        total = lax.dynamic_slice_in_dim(value, self.outer_at * rows, rows, 0)
        for flip in (1, 2, 3):
            piece = lax.dynamic_slice_in_dim(value, (self.outer_at ^ flip) * rows, rows, 0)
            total = total + self.line_move(piece, hops(flip))
        pieces = [total] + [self.line_move(total, hops(flip)) for flip in (1, 2, 3)]
        low, high = self.outer_at % 2 == 0, self.outer_at < 2
        first = [jnp.where(low, pieces[0], pieces[1]), jnp.where(low, pieces[1], pieces[0])]
        second = [jnp.where(low, pieces[2], pieces[3]), jnp.where(low, pieces[3], pieces[2])]
        first, second = jnp.concatenate(first, axis=0), jnp.concatenate(second, axis=0)
        return jnp.concatenate(
            [jnp.where(high, first, second), jnp.where(high, second, first)], axis=0
        )

    def sum_experts(self, value):
        if self.experts != 16:
            return lax.psum(value, "expert")
        columns = value.shape[1] // 2
        x_bit, y_bit = self.inner_at % 2, self.inner_at // 2
        first = self.halve(value[:, :columns], 1, x_bit)
        second = self.halve(value[:, columns:], 2, y_bit)
        first = self.halve(first, 2, y_bit)
        second = self.halve(second, 1, x_bit)
        both = self.line_sum(jnp.concatenate([first, second], axis=1))
        first, second = both[:, :columns], both[:, columns:]
        first = self.unhalve(self.unhalve(first, 2, y_bit), 1, x_bit)
        second = self.unhalve(self.unhalve(second, 1, x_bit), 2, y_bit)
        return jnp.concatenate([first, second], axis=1)

    def sum_small(self, value):
        if self.experts != 16:
            return lax.psum(value, "expert")
        value = value + self.plane_move(value, 1)
        value = value + self.plane_move(value, 2)
        value = value + self.line_move(value, [(a, a ^ 1) for a in range(4)])
        return value + self.line_move(value, [(a, a ^ 2) for a in range(4)])


def rotary_tables(seq_len):
    half_size = HD // 2
    frequency = ROPE_BASE ** (-(jnp.arange(half_size).astype(F32) * 2.0 / HD))
    angles = jnp.arange(seq_len).astype(F32)[:, None] * frequency[None, :]
    zero = jnp.zeros_like(angles)
    cosine, sine = jnp.cos(angles), jnp.sin(angles)
    return (
        jnp.concatenate([cosine] * 4, axis=1),
        jnp.concatenate([-sine, zero] * 2, axis=1),
        jnp.concatenate([zero, sine] * 2, axis=1),
    )


def turn(values, tables, sign):
    cosine, low, high = tables
    parts = []
    for at in range(0, values.shape[1], 128):
        part = values[:, at : at + 128]
        turned = pltpu.roll(part, 96, 1) * low + pltpu.roll(part, 32, 1) * high
        parts.append(part * cosine + sign * turned)
    return jnp.concatenate(parts, axis=1) if len(parts) > 1 else parts[0]


def scores_of(keys, queries, causal):
    raw = dot(keys, queries, 1, 1) * ATTENTION_SCALE
    return raw if causal is None else jnp.where(causal, raw, -1e30)


def attend_kernel(
    at_ref,
    tokens_ref,
    gain_ref,
    cosine_ref,
    low_ref,
    high_ref,
    query_own,
    query_other,
    key_own,
    key_other,
    value_own,
    value_other,
    mixed_ref,
    query_ref,
    key_ref,
    value_ref,
    total_ref,
    normed_ref,
):
    @pl.when(pl.program_id(0) == 0)
    def _():
        inputs = tokens_ref[...].astype(F32)
        scale = lax.rsqrt(jnp.mean(inputs * inputs, axis=1, keepdims=True) + NORM_EPS)
        normed_ref[...] = (inputs * scale * gain_ref[...]).astype(BF)

    half = query_own.shape[0]
    own = normed_ref[:, pl.ds(pl.multiple_of(at_ref[0] * half, half), half)]
    other = normed_ref[:, pl.ds(pl.multiple_of((1 - at_ref[0]) * half, half), half)]
    tables = (cosine_ref[...], low_ref[...], high_ref[...])

    def project(first, second):
        return dot(own, first[...]) + dot(other, second[...])

    queries = turn(project(query_own, query_other), tables, 1.0).astype(BF)
    keys = turn(project(key_own, key_other), tables, 1.0).astype(BF)
    values = project(value_own, value_other).astype(BF)
    query_ref[...] = queries
    key_ref[...] = keys
    value_ref[...] = values
    seq_len = queries.shape[0]
    tile = seq_len // 2
    causal = lax.broadcasted_iota(jnp.int32, (tile, tile), 0) <= lax.broadcasted_iota(
        jnp.int32, (tile, tile), 1
    )
    heads = queries.shape[1] // HD
    group = heads // (keys.shape[1] // HD)
    columns = []
    for head in range(heads):
        shared = head // group
        query = queries[:, head * HD : (head + 1) * HD]
        key = keys[:, shared * HD : (shared + 1) * HD]
        value = values[:, shared * HD : (shared + 1) * HD]
        rows = []
        for row in range(2):
            block = query[row * tile : (row + 1) * tile]
            scores = [
                scores_of(key[at * tile : (at + 1) * tile], block, causal if at == row else None)
                for at in range(row + 1)
            ]
            top = jnp.max(scores[0], axis=0, keepdims=True)
            for extra in scores[1:]:
                top = jnp.maximum(top, jnp.max(extra, axis=0, keepdims=True))
            shifted = [jnp.exp(part - top) for part in scores]
            total = sum(jnp.sum(part, axis=0, keepdims=True) for part in shifted)
            mixed = sum(
                dot(value[at * tile : (at + 1) * tile], shifted[at].astype(BF), 0, 0)
                for at in range(row + 1)
            )
            rows.append(mixed / total)
            total_ref[0, head : head + 1, row * tile : (row + 1) * tile] = top + jnp.log(total)
        columns.append(jnp.concatenate(rows, axis=1))
    mixed_ref[...] = jnp.concatenate(columns, axis=0).T.astype(BF)


def attend(part_at, tokens, gain, tables, own, other, key_total):
    seq_len, width = tokens.shape
    half, columns = own.shape
    inner_total = columns - 2 * key_total
    steps = key_total // 128
    wide = inner_total // steps

    def fixed(shape):
        return pl.BlockSpec(shape, lambda g, at: (0,) * len(shape))

    def column(rows, size, start):
        return pl.BlockSpec((rows, size), lambda g, at: (0, start // size + g))

    weight_specs = []
    for size, start in ((wide, 0), (128, inner_total), (128, inner_total + key_total)):
        weight_specs += [column(half, size, start)] * 2
    return pl.pallas_call(
        attend_kernel,
        grid_spec=pltpu.PrefetchScalarGridSpec(
            num_scalar_prefetch=1,
            grid=(steps,),
            in_specs=[fixed((seq_len, width)), fixed((1, width))]
            + [fixed((seq_len, 128))] * 3
            + weight_specs,
            out_specs=[
                column(seq_len, wide, 0),
                column(seq_len, wide, 0),
                column(seq_len, 128, 0),
                column(seq_len, 128, 0),
                pl.BlockSpec((1, 8, seq_len), lambda g, at: (g, 0, 0)),
            ],
            scratch_shapes=[pltpu.VMEM((seq_len, width), BF)],
        ),
        out_shape=[
            jax.ShapeDtypeStruct((seq_len, inner_total), BF),
            jax.ShapeDtypeStruct((seq_len, inner_total), BF),
            jax.ShapeDtypeStruct((seq_len, key_total), BF),
            jax.ShapeDtypeStruct((seq_len, key_total), BF),
            jax.ShapeDtypeStruct((steps, 8, seq_len), F32),
        ],
        cost_estimate=pl.CostEstimate(
            flops=2 * seq_len * width * columns + 2 * inner_total * seq_len * seq_len,
            transcendentals=inner_total // HD * seq_len * seq_len,
            bytes_accessed=8 << 20,
        ),
        name="attend",
    )(part_at, tokens, gain, *tables, own, other, own, other, own, other)


def attend_back_kernel(
    cosine_ref,
    low_ref,
    high_ref,
    query_in,
    key_in,
    value_in,
    total_ref,
    grad_in,
    query_out,
    key_out,
    value_out,
):
    tables = (cosine_ref[...], low_ref[...], high_ref[...])
    queries, keys, values, grads = query_in[...], key_in[...], value_in[...], grad_in[...]
    seq_len = queries.shape[0]
    tile = seq_len // 2
    causal = lax.broadcasted_iota(jnp.int32, (tile, tile), 0) <= lax.broadcasted_iota(
        jnp.int32, (tile, tile), 1
    )
    heads = queries.shape[1] // HD
    kv_heads = keys.shape[1] // HD
    group = heads // kv_heads
    query_columns, key_columns, value_columns = [], [], []
    for shared in range(kv_heads):
        key = keys[:, shared * HD : (shared + 1) * HD]
        value = values[:, shared * HD : (shared + 1) * HD]
        key_grads, value_grads = [0.0, 0.0], [0.0, 0.0]
        for head in range(shared * group, (shared + 1) * group):
            query = queries[:, head * HD : (head + 1) * HD]
            grad = grads[:, head * HD : (head + 1) * HD]
            rows = []
            for row in range(2):
                span = slice(row * tile, (row + 1) * tile)
                block, outer = query[span], grad[span]
                total = total_ref[0, head : head + 1, span]
                weights, terms, inner = [], [], 0.0
                for at in range(row + 1):
                    part = slice(at * tile, (at + 1) * tile)
                    scores = scores_of(key[part], block, causal if at == row else None)
                    weight = jnp.exp(scores - total)
                    term = dot(value[part], outer, 1, 1)
                    inner = inner + jnp.sum(weight * term, axis=0, keepdims=True)
                    weights.append(weight)
                    terms.append(term)
                query_grad = 0.0
                for at in range(row + 1):
                    part = slice(at * tile, (at + 1) * tile)
                    raw = (weights[at] * (terms[at] - inner) * ATTENTION_SCALE).astype(BF)
                    value_grads[at] = value_grads[at] + dot(weights[at].astype(BF), outer)
                    key_grads[at] = key_grads[at] + dot(raw, block)
                    query_grad = query_grad + dot(key[part], raw, 0, 0)
                rows.append(query_grad)
            query_columns.append(jnp.concatenate(rows, axis=1))
        key_columns.append(jnp.concatenate(key_grads, axis=0))
        value_columns.append(jnp.concatenate(value_grads, axis=0))
    query_grads = jnp.concatenate(query_columns, axis=0).T
    query_out[...] = turn(query_grads, tables, -1.0).astype(BF)
    key_out[...] = turn(jnp.concatenate(key_columns, axis=1), tables, -1.0).astype(BF)
    value_out[...] = jnp.concatenate(value_columns, axis=1).astype(BF)


def attend_back(tables, queries, keys, values, totals, grads):
    seq_len, inner_total = queries.shape
    key_total = keys.shape[1]
    steps = key_total // 128
    wide = inner_total // steps
    fixed = pl.BlockSpec((seq_len, 128), lambda g: (0, 0))
    broad = pl.BlockSpec((seq_len, wide), lambda g: (0, g))
    narrow = pl.BlockSpec((seq_len, 128), lambda g: (0, g))
    return pl.pallas_call(
        attend_back_kernel,
        grid=(steps,),
        in_specs=[fixed] * 3
        + [broad, narrow, narrow, pl.BlockSpec((1, 8, seq_len), lambda g: (g, 0, 0)), broad],
        out_specs=[broad, narrow, narrow],
        out_shape=[
            jax.ShapeDtypeStruct((seq_len, inner_total), BF),
            jax.ShapeDtypeStruct((seq_len, key_total), BF),
            jax.ShapeDtypeStruct((seq_len, key_total), BF),
        ],
        cost_estimate=pl.CostEstimate(
            flops=10 * inner_total * seq_len * seq_len,
            transcendentals=inner_total // HD * seq_len * seq_len,
            bytes_accessed=8 << 20,
        ),
        name="attend_back",
    )(*tables, queries, keys, values, totals, grads)


def experts_kernel(count, carried, at_ref, *refs):
    rows_ref, grads_ref, gates_ref = refs[:3]
    weights = refs[3 : 3 + 4 * count]
    rest = refs[3 + 4 * count :]
    if carried:
        mixture_in, grad_in = rest[:2]
        rest = rest[2:]
    mixture_ref, grad_ref, gate_ref, scaled_ref, pre_ref = rest
    half = weights[0].shape[0]
    hidden_width = weights[0].shape[1] // 2
    own = pl.ds(pl.multiple_of(at_ref[0] * half, half), half)
    other = pl.ds(pl.multiple_of((1 - at_ref[0]) * half, half), half)
    rows_own, rows_other = rows_ref[:, own], rows_ref[:, other]
    grads_own, grads_other = grads_ref[:, own], grads_ref[:, other]
    if carried:
        totals = [
            mixture_in[:, own].astype(F32),
            mixture_in[:, other].astype(F32),
            grad_in[:, own].astype(F32),
            grad_in[:, other].astype(F32),
        ]
    else:
        totals = [0.0] * 4
    for at in range(count):
        up_own, up_other, down_own, down_other = weights[4 * at : 4 * at + 4]
        pre = dot(rows_own, up_own[...]) + dot(rows_other, up_other[...])
        back = dot(grads_own, down_own[...], 1, 1) + dot(grads_other, down_other[...], 1, 1)
        gate_pre, up_pre = pre[:, :hidden_width], pre[:, hidden_width:]
        sigmoid = 1.0 / (1.0 + jnp.exp(-gate_pre))
        active = gate_pre * sigmoid
        hidden = active * up_pre
        factor = RESIDUAL_SCALE * gates_ref[:, at : at + 1]
        gate_ref[:, at : at + 1] = RESIDUAL_SCALE * jnp.sum(hidden * back, axis=1, keepdims=True)
        scaled = (hidden * factor).astype(BF)
        back = back * factor
        grad_gate = back * up_pre * sigmoid * (1.0 + gate_pre * (1.0 - sigmoid))
        grad_pre = jnp.concatenate([grad_gate, back * active], axis=1).astype(BF)
        scaled_ref[at] = scaled
        pre_ref[at] = grad_pre
        totals[0] = totals[0] + dot(scaled, down_own[...])
        totals[1] = totals[1] + dot(scaled, down_other[...])
        totals[2] = totals[2] + dot(grad_pre, up_own[...], 1, 1)
        totals[3] = totals[3] + dot(grad_pre, up_other[...], 1, 1)
    mixture_ref[:, own] = totals[0].astype(BF)
    mixture_ref[:, other] = totals[1].astype(BF)
    grad_ref[:, own] = totals[2].astype(BF)
    grad_ref[:, other] = totals[3].astype(BF)


def experts_pass(part_at, rows, grads, gates, weights, carried=None, tile=512):
    total_rows, width = rows.shape
    count = len(weights)
    half, double = weights[0][0].shape
    hidden_width = double // 2

    def row(size):
        return pl.BlockSpec((tile, size), lambda r, at: (r, 0))

    def stack(size):
        return pl.BlockSpec((count, tile, size), lambda r, at: (0, r, 0))

    def fixed(shape):
        return pl.BlockSpec(shape, lambda r, at: (0, 0), pipeline_mode=pl.Buffered(1))

    weight_specs, operands = [], []
    for up_own, up_other, down_own, down_other in weights:
        operands += [up_own, up_other, down_own, down_other]
        weight_specs += [fixed(up_own.shape)] * 2 + [fixed(down_own.shape)] * 2
    operands = [rows, grads, gates] + operands + list(carried or ())
    return pl.pallas_call(
        partial(experts_kernel, count, carried is not None),
        grid_spec=pltpu.PrefetchScalarGridSpec(
            num_scalar_prefetch=1,
            grid=(total_rows // tile,),
            in_specs=[row(width), row(width), row(count)]
            + weight_specs
            + ([row(width)] * 2 if carried else []),
            out_specs=[row(width), row(width), row(count), stack(hidden_width), stack(double)],
        ),
        out_shape=[
            jax.ShapeDtypeStruct((total_rows, width), BF),
            jax.ShapeDtypeStruct((total_rows, width), BF),
            jax.ShapeDtypeStruct((total_rows, count), F32),
            jax.ShapeDtypeStruct((count, total_rows, hidden_width), BF),
            jax.ShapeDtypeStruct((count, total_rows, double), BF),
        ],
        compiler_params=pltpu.CompilerParams(vmem_limit_bytes=56 << 20),
        cost_estimate=pl.CostEstimate(
            flops=12 * count * total_rows * width * hidden_width,
            transcendentals=count * total_rows * hidden_width,
            bytes_accessed=count * (6 << 20) + 16 * total_rows * width,
        ),
        name="experts",
    )(part_at, *operands)


def body(
    tokens,
    routes,
    cotangent,
    attention_gain,
    query_weight,
    key_weight,
    value_weight,
    output_weight,
    router_weight,
    mixture_gain,
    expert_gate,
    expert_up,
    expert_down,
):
    net = Net()
    seq_len, model_width = tokens.shape
    expert_total = router_weight.shape[1]
    hidden_width = expert_gate.shape[2]
    inner_total = query_weight.shape[1]
    key_total = key_weight.shape[1]

    projections = jnp.concatenate([query_weight, key_weight, value_weight], axis=1)
    part_at = (net.part_at if net.parts == 2 else jnp.zeros((), jnp.int32)).reshape(1)
    own_qkv, other_qkv = net.halves(projections, 0)
    weight_output = net.gather_parts(output_weight, 0)
    small = jnp.concatenate(
        [
            router_weight.astype(F32).T,
            attention_gain.astype(F32)[None],
            mixture_gain.astype(F32)[None],
        ],
        axis=0,
    )
    small = net.gather_parts(small, 1)
    router_wide = small[:expert_total].T
    weight_router = router_wide.astype(BF)
    gain_one, gain_two = small[expert_total], small[expert_total + 1]

    gate_up = jnp.concatenate([expert_gate[0], expert_up[0]], axis=1)
    line_gate_up = net.gather_line(gate_up)
    line_down = net.gather_line(expert_down[0])
    grad_blocks = net.gather_plane(cotangent)

    inputs = tokens.astype(F32)
    scale_one = lax.rsqrt(jnp.mean(inputs * inputs, axis=1, keepdims=True) + NORM_EPS)
    unit_one = inputs * scale_one
    normed_one = (unit_one * gain_one).astype(BF)
    tables = rotary_tables(seq_len)
    mixed, query_rot, key_rot, value_rows, totals = attend(
        part_at, tokens, gain_one[None], tables, own_qkv, other_qkv, key_total
    )
    middle = inputs + RESIDUAL_SCALE * dot(mixed, weight_output)
    scale_two = lax.rsqrt(jnp.mean(middle * middle, axis=1, keepdims=True) + NORM_EPS)
    unit_two = middle * scale_two
    normed_two = (unit_two * gain_two).astype(BF)
    row_blocks = net.gather_plane(normed_two)

    logits = dot(weight_router, normed_two, 0, 1)
    chosen = jnp.any(
        routes.T[None] == jnp.arange(expert_total)[:, None, None], axis=1
    )
    shifted = jnp.where(chosen, logits, -1e30)
    shifted = jnp.where(chosen, jnp.exp(shifted - jnp.max(shifted, axis=0, keepdims=True)), 0.0)
    gates = shifted / jnp.sum(shifted, axis=0, keepdims=True)
    gate_blocks = [gates] + [net.plane_move(gates, flip) for flip in range(1, net.inner)]

    order = net.line_order()
    rows = jnp.concatenate(row_blocks, axis=0)
    grads = jnp.concatenate(grad_blocks, axis=0)
    gate_columns = jnp.stack(
        [
            jnp.concatenate(
                [
                    lax.dynamic_index_in_dim(
                        block, at * net.inner + net.inner_at, 0, keepdims=False
                    )
                    for block in gate_blocks
                ]
            )
            for at in order
        ]
    )
    weights = []
    for at in range(OUTER):
        weights.append(net.halves(line_gate_up[at], 0) + net.halves(line_down[at], 1))
    gate_rows = gate_columns.T
    mixture, grad_rows, gates_near, *near = experts_pass(
        part_at, rows, grads, gate_rows[:, :2], weights[:2]
    )
    mixture, grad_rows, gates_far, *far = experts_pass(
        part_at, rows, grads, gate_rows[:, 2:], weights[2:], (mixture, grad_rows)
    )
    grad_gates = jnp.concatenate([gates_near, gates_far], axis=1).T
    grad_weights = []
    for scaled, grad_pre in (near, far):
        for at in range(2):
            grad_weights.append(
                (
                    net.scatter_parts(dot(rows, grad_pre[at], 0, 0).astype(BF), 0),
                    net.scatter_parts(dot(scaled[at], grads, 0, 0).astype(BF), 1),
                )
            )

    def split(value):
        return [value[at * seq_len : (at + 1) * seq_len] for at in range(net.inner)]

    grad_normed_two = net.scatter_plane(split(grad_rows))
    added = net.scatter_plane(split(mixture))
    grad_gate_up = net.scatter_line(*[pair[0] for pair in grad_weights])
    grad_down = net.scatter_line(*[pair[1] for pair in grad_weights])

    gate_terms = grad_gates.reshape(OUTER, net.inner, seq_len)
    places = jnp.stack(order)
    by_outer = jnp.zeros_like(gate_terms).at[places].set(gate_terms)
    received = [by_outer[:, 0]] + [
        net.plane_move(by_outer[:, flip], flip) for flip in range(1, net.inner)
    ]
    received = jnp.stack(received, axis=1)
    flips = jnp.arange(net.inner) ^ net.inner_at
    gate_grads = received[:, flips].reshape(expert_total, seq_len)
    grad_logits = gates * (gate_grads - jnp.sum(gates * gate_grads, axis=0, keepdims=True))
    output = (middle + added).astype(BF)

    grad_out = cotangent.astype(F32)
    grad_normed_two = grad_normed_two + lax.dot_general(
        grad_logits, router_wide, (((0,), (1,)), ((), ())), precision=HIGHEST
    )
    grad_router = lax.dot_general(
        grad_logits, normed_two.astype(F32), (((1,), (0,)), ((), ())), precision=HIGHEST
    )
    grad_unit_two = grad_normed_two * gain_two
    grad_gain_two = jnp.sum(grad_normed_two * unit_two, axis=0)
    grad_middle = grad_out + scale_two * (
        grad_unit_two - unit_two * jnp.mean(grad_unit_two * unit_two, axis=1, keepdims=True)
    )
    grad_attention = (RESIDUAL_SCALE * grad_middle).astype(BF)
    grad_output_weight = dot(mixed, grad_attention, 0, 0).astype(BF)
    total_output = net.sum_experts(net.scatter_parts(grad_output_weight, 0))
    grad_mixed = dot(grad_attention, weight_output, 1, 1).astype(BF)
    grad_query, grad_key, grad_value = attend_back(
        tables, query_rot, key_rot, value_rows, totals, grad_mixed
    )
    grad_qkv = jnp.concatenate([grad_query, grad_key, grad_value], axis=1)
    grad_qkv_weight = dot(normed_one, grad_qkv, 0, 0).astype(BF)
    total_qkv = net.sum_experts(net.scatter_parts(grad_qkv_weight, 0))
    first = part_at[0] == 0
    low_part, high_part = dot(grad_qkv, own_qkv, 1, 1), dot(grad_qkv, other_qkv, 1, 1)
    grad_normed_one = jnp.concatenate(
        [jnp.where(first, low_part, high_part), jnp.where(first, high_part, low_part)], axis=1
    )
    grad_unit_one = grad_normed_one * gain_one
    grad_gain_one = jnp.sum(grad_normed_one * unit_one, axis=0)
    grad_inputs = grad_middle + scale_one * (
        grad_unit_one - unit_one * jnp.mean(grad_unit_one * unit_one, axis=1, keepdims=True)
    )
    small_grads = jnp.concatenate([grad_router, grad_gain_one[None], grad_gain_two[None]], axis=0)
    small_grads = net.sum_small(net.scatter_parts(small_grads, 1))
    return (
        output,
        grad_inputs,
        small_grads[expert_total],
        total_qkv[:, :inner_total].astype(F32),
        total_qkv[:, inner_total : inner_total + key_total].astype(F32),
        total_qkv[:, inner_total + key_total :].astype(F32),
        total_output.astype(F32),
        small_grads[:expert_total].T,
        small_grads[expert_total + 1],
        grad_gate_up[None, :, :hidden_width],
        grad_gate_up[None, :, hidden_width:],
        grad_down[None],
    )


def solution(mesh):
    both, one = P(("expert", "fsdp"), None), P("fsdp", None)
    rows, columns = P("expert", "fsdp", None), P("expert", None, "fsdp")
    return jax.shard_map(
        body,
        mesh=mesh,
        in_specs=(both, both, both, P("fsdp"), one, one, one, one, one, P("fsdp"), rows, rows, columns),
        out_specs=(both, both, P("fsdp"), one, one, one, one, one, P("fsdp"), rows, rows, columns),
        check_vma=False,
    )
```
